256 devices in a mesh: replica: 32 (over z_lo, x, core), shard: 8 (over y, z_hi).
Axes of the slice: x: 4, y: 4, z: 8 (z_hi: 2, z_lo: 4; z = z_hi * 4 + z_lo), core: 2. Of those that a mesh axis runs over, the one named last changes fastest.
Arguments:
- normed: bfloat16 [65536, 8192], P(('replica', 'shard')), may hold values from -96 to 96
- out_grads: bfloat16 [65536, 1024], P(('replica', 'shard')), may hold values from -4 to 4
- weight: float32 [8192, 1024], P(('replica', 'shard')), may hold values from -6 to 6
- moment: float32 [8192, 1024], P(('replica', 'shard')), may hold values from -6 to 6
- variance: float32 [8192, 1024], P(('replica', 'shard')), may hold values from 0.5 to 8
Outputs:
- new_weight: float32 [8192, 1024], P(('replica', 'shard'))
- new_moment: float32 [8192, 1024], P(('replica', 'shard'))
- new_variance: float32 [8192, 1024], P(('replica', 'shard'))
The draws below stay inside these ranges and needn't reach their ends.
All inputs are finite; a program needn't handle non-finite values.
Results may differ from the reference program's by a relative error of at most 0.002.
Values may be sent and summed in bfloat16 or wider, within the bound.
A program may use at most 128 MiB of HBM per device.

```python
import math
import jax
import jax.numpy as jnp
from jax import lax

D = 8192
TOK_DEV = 256
STEP = 10
C = 1024
TOKENS = 65536
N_REPLICA = 32
N_SHARD = 8


def draw_normed(key, part):
    key_base = jax.random.fold_in(jax.random.fold_in(key, 11), 0)
    key_scale = jax.random.fold_in(jax.random.fold_in(key, 11), 1)
    key_pair = jax.random.fold_in(jax.random.fold_in(key, 11), 3)
    spread = jax.random.uniform(key_scale, (D,), jnp.float32)
    ramp = 1.0 + 2.0 * jnp.arange(D, dtype=jnp.float32) / (D - 1)
    scale = ramp * jnp.exp(spread * math.log(10.0)) / 10.0
    blocks = TOKENS // TOK_DEV
    width = D // blocks
    pairing = jax.random.permutation(key_pair, blocks)
    tok_block = jnp.arange(TOKENS, dtype=jnp.int32) // TOK_DEV
    col_block = jnp.arange(D, dtype=jnp.int32) // width
    paired = pairing[tok_block][:, None] == col_block[None, :]
    factor = jnp.where(paired, jnp.float32(8.0), jnp.float32(1.0))
    base = jnp.clip(jax.random.normal(key_base, (TOKENS, D), jnp.float32), -4.0, 4.0)
    return (base * scale[None, :] * factor).astype(jnp.bfloat16)


def draw_out_grads(key, part):
    key_base, key_scale = jax.random.split(jax.random.fold_in(key, 12), 2)
    spread = jax.random.uniform(key_scale, (C,), jnp.float32)
    scale = jnp.exp(spread * math.log(10.0)) / 10.0
    base = jnp.clip(jax.random.normal(key_base, (TOKENS, C), jnp.float32), -4.0, 4.0)
    return (base * scale[None, :]).astype(jnp.bfloat16)


def shard_levels(rng, extent, pieces, low, top_value):
    level, own = 1.0, jax.random.fold_in(rng, 6)
    for dim, shards_of in pieces:
        draws = jnp.exp(jax.random.uniform(jax.random.fold_in(own, dim), (shards_of,), jnp.float32, low / len(pieces), top_value / len(pieces)))
        level = level * jnp.repeat(draws, extent[dim] // shards_of).reshape([-1 if axis == dim else 1 for axis in range(len(extent))])
    return level


def bell_draw(key, extent, deviation, most, cuts=(), kind=jnp.bfloat16):
    values = jax.random.normal(key, extent, jnp.float32) * deviation
    if len(cuts) > 0:
        values = shard_levels(key, extent, cuts, -0.22, 0.18) * values
    return jnp.clip(values, min=-most, max=most).astype(kind)


def setup_inputs(seed: int = 0) -> dict:
    key_of = jax.random.split(jax.random.key(seed), 6)
    return {
        "normed": draw_normed(jax.random.fold_in(key_of[5], 71), 0),
        "out_grads": draw_out_grads(jax.random.fold_in(key_of[5], 71), 0),
        "weight": bell_draw(key_of[2], (D, C), 1.0, 6.0, ((0, 256),), jnp.float32),
        "moment": bell_draw(key_of[3], (D, C), 1.0, 6.0, ((0, 256),), jnp.float32),
        "variance": jnp.clip(jnp.exp(math.log(8.0) - 2.7725887 * jax.random.uniform(key_of[4], (D, C), jnp.float32) ** shard_levels(key_of[4], (D, C), ((0, 256),), -0.2, 0.2)), 0.5, 8.0),
    }


def reference(normed, out_grads, weight, moment, variance):
    blocks = N_REPLICA * N_SHARD
    inputs = normed.reshape(blocks, TOK_DEV, D)
    grads = out_grads.reshape(blocks, TOK_DEV, C)

    def accumulate(total, pair):
        left = pair[0].astype(jnp.float32)
        right = pair[1].astype(jnp.float32)
        part = jnp.dot(left.T, right, precision=lax.Precision.HIGHEST, preferred_element_type=jnp.float32)
        part = lax.optimization_barrier(part.astype(jnp.bfloat16)).astype(jnp.float32)
        return (total + part, None)
    grad, unused = lax.scan(accumulate, jnp.zeros((D, C), jnp.float32), (inputs, grads))
    squares = jnp.sum(grad * grad)
    limit = jnp.sqrt(jnp.float32(D * C))
    clip = jnp.minimum(jnp.float32(1.0), limit / (jnp.sqrt(squares) + 1e-06))
    scaled = clip * grad
    new_moment = 0.9 * moment + 0.1 * scaled
    new_variance = 0.95 * variance + 0.05 * scaled * scaled
    first = new_moment / (1.0 - 0.9 ** STEP)
    second = new_variance / (1.0 - 0.95 ** STEP)
    new_weight = weight - 0.01 * (first / (jnp.sqrt(second) + 1e-08) + 0.1 * weight)
    return (new_weight, new_moment, new_variance)
```

```python
import jax
import jax.numpy as jnp
from jax import lax
from jax.experimental import pallas as pl
from jax.experimental.pallas import tpu as pltpu
from jax.sharding import Mesh
from jax.sharding import PartitionSpec as P

STEP = 10
AXES = ("z_lo", "x", "core", "y", "z_hi")
SIZES = (4, 4, 2, 4, 2)
MESH_ID = pl.DeviceIdType.MESH
F32, BF16 = jnp.float32, jnp.bfloat16
CX, CY, CZ = 384, 256, 384
BLOCK = 256
ROWS = 32
TOK = 256


class Sems:
    def __init__(self, send, recv):
        self.send, self.recv, self.used, self.sent = send, recv, 0, []

    def take(self):
        self.used += 1
        return self.send.at[self.used - 1], self.recv.at[self.used - 1]


class Ring:
    def __init__(self, n, me, device, view, length, landing, sems):
        self.n, self.me, self.device, self.view = n, me, device, view
        self.length, self.landing, self.sems = length, landing, sems
        self.copies = {}
        for way in (0, 1):
            for half in (0, 1):
                for hop in range(1, self.reach(way, half) + 1):
                    self.copies[way, half, hop] = self.copy(way, half, hop)

    def reach(self, way, half):
        return self.n // 2 if way == half else self.n // 2 - 1

    def slot(self, way, half, hop):
        return hop - 1 if half == 0 else self.reach(way, 0) + hop - 1

    def dest(self, way, hop):
        return lax.rem(self.me + (hop if way == 0 else self.n - hop), self.n)

    def copy(self, way, half, hop):
        send, recv = self.sems.take()
        return pltpu.make_async_remote_copy(
            src_ref=self.view(self.dest(way, hop), half),
            dst_ref=self.landing.at[way, self.slot(way, half, hop)],
            send_sem=send,
            recv_sem=recv,
            device_id=self.device(way),
            device_id_type=MESH_ID,
        )

    def send(self, way, half, hop):
        self.copies[way, half, hop].start()
        self.sems.sent.append(self.copies[way, half, hop])

    def first(self):
        for way in (0, 1):
            self.send(way, way, self.n // 2)

    def direct(self):
        for way in (0, 1):
            self.send(way, 1 - way, self.n // 2 - 1)

    def onward(self, far, hop):
        for way in (0, 1):
            half = way if far else 1 - way
            self.copies[way, half, hop + 1].wait_recv()
            target = self.view(self.dest(way, hop), half)
            came = self.landing.at[way, self.slot(way, half, hop + 1)]

            def add(i, _):
                target[i] = (target[i].astype(F32) + came[i].astype(F32)).astype(BF16)
                return 0

            lax.fori_loop(0, self.length, add, 0)
            self.send(way, half, hop)

    def last(self):
        for half in (0, 1):
            target = self.view(self.me, half)
            came = []
            for way in (0, 1):
                self.copies[way, half, 1].wait_recv()
                came.append(self.landing.at[way, self.slot(way, half, 1)])

            def add(i, _):
                total = target[i].astype(F32) + came[0][i].astype(F32)
                target[i] = (total + came[1][i].astype(F32)).astype(BF16)
                return 0

            lax.fori_loop(0, self.length, add, 0)


class Direct:
    def __init__(self, n, me, device, source, landing, sems):
        self.sems, self.copies = sems, []
        for off in range(1, n):
            dest = lax.rem(me + off, n)
            send, recv = sems.take()
            self.copies.append(
                pltpu.make_async_remote_copy(
                    src_ref=source(dest),
                    dst_ref=landing.at[off - 1],
                    send_sem=send,
                    recv_sem=recv,
                    device_id=device(dest),
                    device_id_type=MESH_ID,
                )
            )

    def start(self):
        for copy in self.copies:
            copy.start()
            self.sems.sent.append(copy)

    def arrive(self):
        for copy in self.copies:
            copy.wait_recv()


def kernel(
    normed, out_grads, out, lhs, rhs, px, py, pz, lx1, ly1, lz1, lx2, ly2, lz2, lx3, ly3, lz3,
    square, sqz, sqy, sqx, sqc, send_sem, recv_sem, load_sem, in_send, in_recv,
):
    x, y, core = lax.axis_index("x"), lax.axis_index("y"), lax.axis_index("core")
    z_lo, z_hi = lax.axis_index("z_lo"), lax.axis_index("z_hi")
    z = z_hi * 4 + z_lo
    other = 1 - core

    def at_x(i):
        return {"x": i}

    def at_y(i):
        return {"y": i}

    def at_z(i):
        return {"z_hi": i // 4, "z_lo": lax.rem(i, 4)}

    def step_on(place, n, me):
        return lambda way: place(lax.rem(me + (1 if way == 0 else n - 1), n))

    def columns(j, c):
        return pl.ds(pl.multiple_of((2 * j + c) * BLOCK, BLOCK), BLOCK)

    def own_load(j):
        return pltpu.make_async_copy(
            normed.at[:, columns(j, core)], lhs.at[j, pl.ds(0, TOK)], load_sem.at[j]
        )

    def partner_send(j):
        return pltpu.make_async_remote_copy(
            src_ref=normed.at[:, columns(j, other)],
            dst_ref=lhs.at[j, pl.ds(TOK, TOK)],
            send_sem=in_send.at[j],
            recv_sem=in_recv.at[j],
            device_id={"core": other},
            device_id_type=MESH_ID,
        )

    far_x = lax.rem(x + 2, 4)

    def block_a(i):
        return i * 4 + far_x

    def block_b(i):
        return z_lo * 4 + lax.rem(x + 3 + i, 4)

    def block_c(i):
        return lax.rem(z_lo + 1 + i // 3, 4) * 4 + lax.rem(x + 3 + lax.rem(i, 3), 4)

    groups = ((block_a, 4), (block_b, 3), (block_c, 9))

    grads_load = pltpu.make_async_copy(out_grads, rhs.at[pl.ds(0, TOK)], load_sem.at[16])
    grads_send = pltpu.make_async_remote_copy(
        src_ref=out_grads,
        dst_ref=rhs.at[pl.ds(TOK, TOK)],
        send_sem=in_send.at[16],
        recv_sem=in_recv.at[16],
        device_id={"core": other},
        device_id_type=MESH_ID,
    )

    barrier = pltpu.get_barrier_semaphore()
    neighbours = [{"core": other}]
    for place, n, me in ((at_x, 4, x), (at_y, 4, y), (at_z, 8, z)):
        neighbours += [step_on(place, n, me)(0), step_on(place, n, me)(1)]
    for device in neighbours:
        pl.semaphore_signal(barrier, inc=1, device_id=device, device_id_type=MESH_ID)
    grads_load.start()
    for block, count in groups:
        for i in range(count):
            own_load(block(i)).start()
    pl.semaphore_wait(barrier, len(neighbours))
    grads_send.start()
    for block, count in groups:
        for i in range(count):
            partner_send(block(i)).start()

    sems = Sems(send_sem, recv_sem)

    def part(ref, width):
        return lambda lead, start, length: ref.at[lead, pl.ds(start, length)]

    x1 = Ring(4, x, step_on(at_x, 4, x), lambda d, h: px.at[d, pl.ds(16 * h, 16)], 16, lx1, sems)
    y1 = Ring(4, y, step_on(at_y, 4, y), lambda d, h: py.at[d, pl.ds(16 * h, 16)], 16, ly1, sems)
    z1 = Ring(8, z, step_on(at_z, 8, z), lambda d, h: pz.at[d, pl.ds(8 * h, 8)], 8, lz1, sems)
    x2 = Ring(4, y, step_on(at_y, 4, y), lambda d, h: px.at[x, pl.ds(8 * d + 4 * h, 4)], 4, lx2, sems)
    y2 = Ring(4, x, step_on(at_x, 4, x), lambda d, h: py.at[y, pl.ds(8 * d + 4 * h, 4)], 4, ly2, sems)
    z2 = Ring(4, y, step_on(at_y, 4, y), lambda d, h: pz.at[z, pl.ds(4 * d + 2 * h, 2)], 2, lz2, sems)
    x3 = Direct(8, z, at_z, lambda d: px.at[x, 8 * y + d], lx3, sems)
    y3 = Direct(8, z, at_z, lambda d: py.at[y, 8 * x + d], ly3, sems)
    z3 = Direct(4, x, at_x, lambda d: pz.at[z, 4 * y + d], lz3, sems)

    grads_load.wait()
    grads_send.wait_recv()

    def product(j):
        own_load(j).wait()
        partner_send(j).wait_recv()
        zl, xj = j // 4, lax.rem(j, 4)
        total = lax.dot_general(
            lhs[j], rhs[...], (((0,), (0,)), ((), ())), preferred_element_type=F32
        ).astype(BF16)
        for yi in range(4):
            for zh in range(2):
                rows = total[(yi * 2 + zh) * ROWS : (yi * 2 + zh + 1) * ROWS]
                zi = zh * 4 + zl
                px[xj, yi * 8 + zi] = rows[:, :CX]
                py[yi, xj * 8 + zi] = rows[:, CX : CX + CY]
                pz[zi, yi * 4 + xj] = rows[:, CX + CY :]

    def products(block, count):
        def body(i, _):
            product(block(i))
            return 0

        lax.fori_loop(0, count, body, 0)

    products(block_a, 4)
    x1.first()
    products(block_b, 3)
    z1.first()
    products(block_c, 9)
    y1.first()
    x1.direct()
    z1.direct()
    y1.direct()
    z1.onward(True, 3)
    x1.onward(True, 1)
    z1.onward(False, 2)
    y1.onward(True, 1)
    z1.onward(True, 2)
    z1.onward(False, 1)
    x1.last()
    x2.first()
    x2.direct()
    y1.last()
    y2.first()
    y2.direct()
    z1.onward(True, 1)
    x2.onward(True, 1)
    y2.onward(True, 1)
    z1.last()
    z2.first()
    z2.direct()
    x2.last()
    x3.start()
    y2.last()
    y3.start()
    z2.onward(True, 1)
    z2.last()
    z3.start()

    def collect(own, landing, count, lanes):
        total = own[...].astype(F32)
        for i in range(count):
            total = total + landing[i].astype(F32)
        out[:, lanes] = total

    x3.arrive()
    collect(px.at[x, 8 * y + z], lx3, 7, pl.ds(0, CX))
    y3.arrive()
    collect(py.at[y, 8 * x + z], ly3, 7, pl.ds(CX, CY))
    z3.arrive()
    collect(pz.at[z, 4 * y + x], lz3, 3, pl.ds(CX + CY, CZ))

    grad = out[...]
    partial = jnp.zeros((8, 128), F32)
    for r in range(0, ROWS, 8):
        for c in range(0, CX + CY + CZ, 128):
            tile = grad[r : r + 8, c : c + 128]
            partial = partial + tile * tile
    square[0] = partial

    def fold(stage, n, me, place, landing):
        exchange = Direct(n, me, place, lambda d: square.at[stage], landing, sems)
        exchange.start()
        exchange.arrive()
        total = square[stage]
        for i in range(n - 1):
            total = total + landing[i]
        square[stage + 1] = total

    fold(0, 8, z, at_z, sqz)
    fold(1, 4, y, at_y, sqy)
    fold(2, 4, x, at_x, sqx)
    fold(3, 2, core, lambda i: {"core": i}, sqc)
    squares = jnp.sum(square[4], keepdims=True)
    limit = jnp.sqrt(jnp.full((1, 1), 8192.0 * 1024.0, F32))
    clip = jnp.minimum(1.0, limit / (jnp.sqrt(squares) + 1e-06))
    out[...] = out[...] * clip

    for copy in sems.sent:
        copy.wait_send()
    grads_send.wait_send()
    for j in range(16):
        partner_send(j).wait_send()


def scaled_gradient(normed, out_grads):
    def landing(n, length, width):
        return pltpu.VMEM((2, n - 1, length, ROWS, width), BF16)

    def pieces(n, width):
        return pltpu.VMEM((n - 1, ROWS, width), BF16)

    n_sems = 6 + 6 + 14 + 6 + 6 + 6 + 7 + 7 + 3 + 7 + 3 + 3 + 1
    return pl.pallas_call(
        kernel,
        out_shape=jax.ShapeDtypeStruct((ROWS, CX + CY + CZ), F32),
        in_specs=[pl.BlockSpec(memory_space=pl.ANY)] * 2,
        out_specs=pl.BlockSpec(memory_space=pltpu.VMEM),
        scratch_shapes=[
            pltpu.VMEM((16, 2 * TOK, BLOCK), BF16),
            pltpu.VMEM((2 * TOK, CX + CY + CZ), BF16),
            pltpu.VMEM((4, 32, ROWS, CX), BF16),
            pltpu.VMEM((4, 32, ROWS, CY), BF16),
            pltpu.VMEM((8, 16, ROWS, CZ), BF16),
            landing(4, 16, CX),
            landing(4, 16, CY),
            landing(8, 8, CZ),
            landing(4, 4, CX),
            landing(4, 4, CY),
            landing(4, 2, CZ),
            pieces(8, CX),
            pieces(8, CY),
            pieces(4, CZ),
            pltpu.VMEM((5, 8, 128), F32),
            pltpu.VMEM((7, 8, 128), F32),
            pltpu.VMEM((3, 8, 128), F32),
            pltpu.VMEM((3, 8, 128), F32),
            pltpu.VMEM((1, 8, 128), F32),
            pltpu.SemaphoreType.DMA((n_sems,)),
            pltpu.SemaphoreType.DMA((n_sems,)),
            pltpu.SemaphoreType.DMA((17,)),
            pltpu.SemaphoreType.DMA((17,)),
            pltpu.SemaphoreType.DMA((17,)),
        ],
        compiler_params=pltpu.CompilerParams(collective_id=0, has_side_effects=True),
    )(normed, out_grads)


def shards(normed, out_grads, weight, moment, variance):
    scaled = scaled_gradient(normed, out_grads)
    new_moment = 0.9 * moment + 0.1 * scaled
    new_variance = 0.95 * variance + 0.05 * scaled * scaled
    first = new_moment / (1.0 - 0.9**STEP)
    second = new_variance / (1.0 - 0.95**STEP)
    new_weight = weight - 0.01 * (first / (jnp.sqrt(second) + 1e-08) + 0.1 * weight)
    return (new_weight, new_moment, new_variance)


def solution(mesh):
    split = Mesh(mesh.devices.reshape(SIZES), AXES)
    spec = P(AXES, None)
    return jax.shard_map(
        shards, mesh=split, in_specs=(spec,) * 5, out_specs=(spec,) * 3, check_vma=False
    )
```

```python
import jax
import jax.numpy as jnp
from jax import lax
from jax.experimental import pallas as pl
from jax.experimental.pallas import tpu as pltpu
from jax.sharding import Mesh
from jax.sharding import PartitionSpec as P

STEP = 10
AXES = ("z_lo", "x", "core", "y", "z_hi")
SIZES = (4, 4, 2, 4, 2)
MESH_ID = pl.DeviceIdType.MESH
F32, BF16 = jnp.float32, jnp.bfloat16
D, C, TOK, BLOCK, ROWS = 8192, 1024, 256, 256, 32

STREAMS = ("xyz", "yxz", "zxy")
UNITS = (5, 5, 6)
LENGTH = {"x": 4, "y": 4, "z": 8}
FAR_FIRST = {4: (2, 3, 1, 0), 8: (4, 5, 3, 6, 2, 7, 1, 0)}
PRODUCTS_FIRST, PRODUCTS_NEXT, RATE, LATE, ADDS, SLACK = 6.4, 1.95, 93.6e3, 1.5, 0.9e6, 3.0


def ring_length(s, k):
    return LENGTH[STREAMS[s][k]]


def is_ring(s, k):
    return k < 2 or STREAMS[s][2] == "z"


def piece_count(s, k):
    return (ring_length(s, 1), 2, 1)[k]


def piece_length(s, k):
    return (ring_length(s, 2), ring_length(s, 2) // 2, 1)[k]


def reach(n, way, piece):
    return n // 2 if way == piece % 2 else n // 2 - 1


def hops(s, k):
    for piece in range(piece_count(s, k)):
        for way in (0, 1):
            for hop in range(1, reach(ring_length(s, k), way, piece) + 1):
                yield way, piece, hop


def plan():
    tasks = [("g", i) for i in range(4)]
    for s in range(3):
        for k in range(3):
            if is_ring(s, k):
                tasks += [("l", s, k, piece) for piece in range(piece_count(s, k))]
                tasks += [("s", s, k, *which) for which in hops(s, k)]
            else:
                tasks.append(("d", s))
    link, arrive, done, order = {}, {}, {}, []

    def size(s, k):
        return piece_length(s, k) * UNITS[s] * 16 * 128 * 2

    def own(s, k, piece, off):
        if k == 0:
            first, second = STREAMS[s][:2]
            if first == "x":
                return [("g", FAR_FIRST[4].index(off))]
            return [("g", piece if second == "x" else 3)]
        if k == 1:
            return [("l", s, 0, FAR_FIRST[ring_length(s, 1)].index(off))]
        return [("l", s, 1, 0), ("l", s, 1, 1)]

    def fresh(t):
        return t[0] == "s" and t[5] == reach(ring_length(t[1], t[2]), t[3], t[4])

    def filler(t):
        return fresh(t) and t[5] < ring_length(t[1], t[2]) // 2

    def ready(t):
        if t[0] == "g":
            return 0.0 if t[1] == 0 or ("g", t[1] - 1) in done else None
        came = []
        if t[0] == "d":
            need = own(t[1], 2, 0, 0)
        elif t[0] == "s":
            s, k, way, piece, hop = t[1:]
            n = ring_length(s, k)
            need = own(s, k, piece, hop if way == 0 else n - hop)
            came = [] if fresh(t) else [(s, k, way, piece, hop + 1)]
        else:
            s, k, piece = t[1:]
            need = own(s, k, piece, 0)
            came = [(s, k, way, piece, 1) for way in (0, 1)]
        if any(d not in done for d in need) or any(a not in arrive for a in came):
            return None
        at = max([done[d] for d in need] + [arrive[a] for a in came])
        if filler(t):
            at = max(at, link.get((STREAMS[t[1]][t[2]], t[3]), 0.0) - SLACK)
        return at

    def rank(t):
        if t[0] == "d":
            return (0,)
        if t[0] == "s":
            return (3 if filler(t) else 1, -t[2], -t[5], t[4])
        return (2, -t[2], t[3]) if t[0] == "l" else (4, t[1])

    now = 0.0
    while tasks:
        times = {t: ready(t) for t in tasks}
        able = [t for t in tasks if times[t] is not None and times[t] <= now + 1e-9]
        if not able:
            now = min(v for v in times.values() if v is not None)
            continue
        t = min(able, key=rank)
        tasks.remove(t)
        order.append(t)
        if t[0] == "g":
            now = max(now, PRODUCTS_FIRST) if t[1] == 0 else now + PRODUCTS_NEXT
        elif t[0] == "l":
            now += 3 * size(t[1], t[2]) / 4 / ADDS
        elif t[0] == "s":
            s, k, way, piece, hop = t[1:]
            now += 0.0 if fresh(t) else size(s, k) / 2 / ADDS
            key = (STREAMS[s][k], way)
            link[key] = max(now + 0.05, link.get(key, 0.0)) + 2 * size(s, k) / RATE
            arrive[t[1:]] = link[key] + LATE
        done[t] = now
    return order


class Sems:
    def __init__(self, send, recv):
        self.send, self.recv, self.used, self.sent = send, recv, 0, []

    def start(self, copy):
        copy.start()
        self.sent.append(copy)

    def copy(self, source, target, device):
        self.used += 1
        return pltpu.make_async_remote_copy(
            src_ref=source,
            dst_ref=target,
            send_sem=self.send.at[self.used - 1],
            recv_sem=self.recv.at[self.used - 1],
            device_id=device,
            device_id_type=MESH_ID,
        )


class Ring:
    def __init__(self, s, k, me, place, view, landing, sems):
        self.n, self.me, self.view, self.sems = ring_length(s, k), me, view, sems
        self.length, self.copies, self.came = piece_length(s, k), {}, {}
        used = [0, 0]
        for way, piece, hop in hops(s, k):
            slot = landing.at[way, used[way]]
            used[way] += 1
            self.came[way, piece, hop] = slot
            self.copies[way, piece, hop] = sems.copy(
                view(self.dest(way, hop), piece), slot, place(self.dest(way, 1))
            )

    def dest(self, way, hop):
        return lax.rem(self.me + (hop if way == 0 else self.n - hop), self.n)

    def send(self, way, piece, hop):
        if hop < reach(self.n, way, piece):
            self.copies[way, piece, hop + 1].wait_recv()
            target, came = self.view(self.dest(way, hop), piece), self.came[way, piece, hop + 1]

            def add(i, _):
                target[i] = (target[i].astype(F32) + came[i].astype(F32)).astype(BF16)
                return 0

            lax.fori_loop(0, self.length, add, 0)
        self.sems.start(self.copies[way, piece, hop])

    def arrive(self, piece):
        for way in (0, 1):
            self.copies[way, piece, 1].wait_recv()
        return self.came[0, piece, 1], self.came[1, piece, 1]

    def last(self, piece):
        a, b = self.arrive(piece)
        target = self.view(self.me, piece)

        def add(i, _):
            total = target[i].astype(F32) + a[i].astype(F32)
            target[i] = (total + b[i].astype(F32)).astype(BF16)
            return 0

        lax.fori_loop(0, self.length, add, 0)


def kernel(normed, out_grads, out, lhs, rhs, *refs):
    partials, landings = refs[:3], (refs[3:6], refs[6:9], refs[9:12])
    squares, send_sem, recv_sem, load_sem, in_send, in_recv, heard = refs[12:]
    x, y, core = lax.axis_index("x"), lax.axis_index("y"), lax.axis_index("core")
    z_lo, z_hi = lax.axis_index("z_lo"), lax.axis_index("z_hi")
    place_of = {
        "x": lambda i: {"x": i},
        "y": lambda i: {"y": i},
        "z": lambda i: {"z_hi": i // 4, "z_lo": lax.rem(i, 4)},
    }
    here = {"x": x, "y": y, "z": z_hi * 4 + z_lo}
    other = 1 - core

    def columns(j, c):
        return pl.ds(pl.multiple_of((2 * j + c) * BLOCK, BLOCK), BLOCK)

    def own_load(j):
        return pltpu.make_async_copy(
            normed.at[:, columns(j, core)], lhs.at[j, pl.ds(0, TOK)], load_sem.at[j]
        )

    def partner_copy(source, target, j):
        return pltpu.make_async_remote_copy(
            src_ref=source,
            dst_ref=target,
            send_sem=in_send.at[j],
            recv_sem=in_recv.at[j],
            device_id={"core": other},
            device_id_type=MESH_ID,
        )

    def partner_send(j):
        return partner_copy(normed.at[:, columns(j, other)], lhs.at[j, pl.ds(TOK, TOK)], j)

    blocks = [i * 4 + lax.rem(x + off, 4) for off in FAR_FIRST[4] for i in range(4)]
    grads_load = pltpu.make_async_copy(out_grads, rhs.at[pl.ds(0, TOK)], load_sem.at[16])
    grads_send = partner_copy(out_grads, rhs.at[pl.ds(TOK, TOK)], 16)

    barrier = pltpu.get_barrier_semaphore()
    neighbours = [{"core": other}]
    for axis in "xyz":
        for step in (1, LENGTH[axis] - 1):
            neighbours.append(place_of[axis](lax.rem(here[axis] + step, LENGTH[axis])))
    for device in neighbours:
        pl.semaphore_signal(barrier, inc=1, device_id=device, device_id_type=MESH_ID)
    grads_load.start()
    for j in blocks:
        own_load(j).start()
    pl.semaphore_wait(barrier, len(neighbours))
    grads_send.start()
    for j in blocks:
        partner_send(j).start()

    sems = Sems(send_sem, recv_sem)
    firsts = [sum(UNITS[:s]) for s in range(3)]

    def tile(s, i):
        unit = firsts[s] + i
        return slice(unit // 8 * 16, unit // 8 * 16 + 16), slice(unit % 8 * 128, unit % 8 * 128 + 128)

    def views(s):
        ref = partials[s]
        a1, a2, a3 = STREAMS[s]
        n2, n3 = LENGTH[a2], LENGTH[a3]

        def first(dest, piece):
            i2 = lax.rem(here[a2] + FAR_FIRST[n2][piece], n2)
            return ref.at[dest, pl.ds(n3 * i2, n3)]

        def second(dest, piece):
            return ref.at[here[a1], pl.ds(n3 * dest + n3 // 2 * piece, n3 // 2)]

        def third(dest, piece=0):
            return ref.at[here[a1], pl.ds(n3 * here[a2] + dest, 1)]

        return first, second, third

    stages, directs = {}, {}
    for s in range(3):
        for k in range(3):
            axis, view, landing = STREAMS[s][k], views(s)[k], landings[k][s]
            if is_ring(s, k):
                stages[s, k] = Ring(s, k, here[axis], place_of[axis], view, landing, sems)
            else:
                directs[s] = []
                for off in range(1, LENGTH[axis]):
                    dest = lax.rem(here[axis] + off, LENGTH[axis])
                    directs[s].append(sems.copy(view(dest), landing.at[off - 1], place_of[axis](dest)))

    grads_load.wait()
    grads_send.wait_recv()

    def products(i):
        xj = lax.rem(x + FAR_FIRST[4][i], 4)

        def body(zl, _):
            j = zl * 4 + xj
            own_load(j).wait()
            partner_send(j).wait_recv()
            total = lax.dot_general(
                lhs[j], rhs[...], (((0,), (0,)), ((), ())), preferred_element_type=F32
            ).astype(BF16)
            for yi in range(4):
                for zh in range(2):
                    at = {"x": xj, "y": yi, "z": zh * 4 + zl}
                    rows = total[(yi * 2 + zh) * ROWS : (yi * 2 + zh + 1) * ROWS]
                    for s, (a1, a2, a3) in enumerate(STREAMS):
                        for u in range(UNITS[s]):
                            place = at[a2] * LENGTH[a3] + at[a3]
                            partials[s][at[a1], place, u * 16 : u * 16 + 16] = rows[tile(s, u)]
            return 0

        lax.fori_loop(0, 4, body, 0)

    sums = jnp.zeros((8, 128), F32)

    def finish(s, total, sums):
        for u in range(UNITS[s]):
            part = total[u * 16 : u * 16 + 16]
            out[tile(s, u)] = part
            sums = sums + part[:8] * part[:8] + part[8:] * part[8:]
        return sums

    order = plan()
    rounds = [t for t in order if t[:3] == ("l", 2, 0)]
    for t in order:
        if t[0] == "g":
            products(t[1])
        elif t[0] == "d":
            for copy in directs[t[1]]:
                sems.start(copy)
        elif t[0] == "s":
            stages[t[1], t[2]].send(*t[3:])
        elif t[2] < 2:
            stages[t[1], t[2]].last(t[3])
        else:
            ring = stages[t[1], 2]
            a, b = ring.arrive(0)
            total = ring.view(ring.me, 0)[0].astype(F32) + a[0].astype(F32)
            sums = finish(t[1], total + b[0].astype(F32), sums)
        if t == rounds[-1]:
            pl.semaphore_signal(heard, inc=1, device_id={"core": other}, device_id_type=MESH_ID)
    for s, copies in directs.items():
        total = views(s)[2](here[STREAMS[s][2]])[0].astype(F32)
        for i, copy in enumerate(copies):
            copy.wait_recv()
            total = total + landings[2][s][i, 0].astype(F32)
        sums = finish(s, total, sums)
    pl.semaphore_wait(heard, 1)

    def fold(box, part, offsets, place):
        box[0:1] = part
        copies = []
        for i, off in enumerate(offsets):
            copies.append(sems.copy(box.at[pl.ds(0, 1)], box.at[pl.ds(i + 1, 1)], place(off)))
            sems.start(copies[-1])
        for copy in copies:
            copy.wait_recv()
        return jnp.sum(box[...], axis=0, keepdims=True)

    def along_z(off):
        return {**place_of["z"](lax.rem(here["z"] + off[1], 8)), "core": lax.rem(core + off[0], 2)}

    def across(off):
        return {"x": lax.rem(x + off[0], 4), "y": lax.rem(y + off[1], 4)}

    part = jnp.sum(sums, axis=0, keepdims=True)
    part = fold(squares.at[0], part, [(c, i) for i in FAR_FIRST[8] for c in (1, 0)][:-1], along_z)
    part = fold(squares.at[1], part, [(i, k) for i in FAR_FIRST[4] for k in FAR_FIRST[4]][:-1], across)
    total = jnp.sum(part, axis=1, keepdims=True)
    limit = jnp.sqrt(jnp.full((1, 1), float(D * C), F32))
    clip = jnp.minimum(1.0, limit / (jnp.sqrt(total) + 1e-06))
    out[...] = out[...] * clip

    for copy in sems.sent:
        copy.wait_send()
    grads_send.wait_send()
    for j in range(16):
        partner_send(j).wait_send()


def scaled_gradient(normed, out_grads):
    partials, landings, copies = [], [], 30
    for s in range(3):
        n1, n2, n3 = (ring_length(s, k) for k in range(3))
        partials.append(pltpu.VMEM((n1, n2 * n3, UNITS[s] * 16, 128), BF16))
    for k in range(3):
        for s in range(3):
            tail = (piece_length(s, k), UNITS[s] * 16, 128)
            if is_ring(s, k):
                ways = [way for way, _, _ in hops(s, k)]
                landings.append(pltpu.VMEM((2, max(ways.count(0), ways.count(1)), *tail), BF16))
                copies += len(ways)
            else:
                landings.append(pltpu.VMEM((ring_length(s, k) - 1, *tail), BF16))
                copies += ring_length(s, k) - 1
    return pl.pallas_call(
        kernel,
        out_shape=jax.ShapeDtypeStruct((ROWS, C), F32),
        in_specs=[pl.BlockSpec(memory_space=pl.ANY)] * 2,
        out_specs=pl.BlockSpec(memory_space=pltpu.VMEM),
        scratch_shapes=[
            pltpu.VMEM((16, 2 * TOK, BLOCK), BF16),
            pltpu.VMEM((2 * TOK, C), BF16),
            *partials,
            *landings,
            pltpu.VMEM((2, 16, 128), F32),
            pltpu.SemaphoreType.DMA((copies,)),
            pltpu.SemaphoreType.DMA((copies,)),
            pltpu.SemaphoreType.DMA((17,)),
            pltpu.SemaphoreType.DMA((17,)),
            pltpu.SemaphoreType.DMA((17,)),
            pltpu.SemaphoreType.REGULAR,
        ],
        compiler_params=pltpu.CompilerParams(collective_id=0, has_side_effects=True),
    )(normed, out_grads)


def shards(normed, out_grads, weight, moment, variance):
    scaled = scaled_gradient(normed, out_grads)
    new_moment = 0.9 * moment + 0.1 * scaled
    new_variance = 0.95 * variance + 0.05 * scaled * scaled
    first = new_moment / (1.0 - 0.9**STEP)
    second = new_variance / (1.0 - 0.95**STEP)
    new_weight = weight - 0.01 * (first / (jnp.sqrt(second) + 1e-08) + 0.1 * weight)
    return (new_weight, new_moment, new_variance)


def solution(mesh):
    split = Mesh(mesh.devices.reshape(SIZES), AXES)
    spec = P(AXES, None)
    return jax.shard_map(
        shards, mesh=split, in_specs=(spec,) * 5, out_specs=(spec,) * 3, check_vma=False
    )
```

```python
import jax
import jax.numpy as jnp
from jax import lax
from jax.experimental import pallas as pl
from jax.experimental.pallas import tpu as pltpu
from jax.sharding import Mesh
from jax.sharding import PartitionSpec as P

STEP = 10
AXES = ("z_lo", "x", "core", "y", "z_hi")
SIZES = (4, 4, 2, 4, 2)
MESH_ID = pl.DeviceIdType.MESH
F32, BF16 = jnp.float32, jnp.bfloat16
D, C, TOK, BLOCK, ROWS = 8192, 1024, 256, 256, 32

STREAMS = ("xzy", "yzx", "zxy")
UNITS = (6, 6, 4)
LENGTH = {"x": 4, "y": 4, "z": 8}
FAR_FIRST = {4: (2, 3, 1, 0), 8: (4, 5, 3, 6, 2, 7, 1, 0)}
GROUPS = (4, 3, 3, 3, 3)
LATER = {1: 2, 3: 3, 2: 4}
PRODUCTS_FIRST, PRODUCTS_NEXT, RATE, LATE, ADDS, SLACK = 6.4, 1.45, 93.6e3, 2.0, 0.9e6, 3.0


def ring_length(s, k):
    return LENGTH[STREAMS[s][k]]


def is_ring(s, k):
    return k < 2 or STREAMS[s][2] == "z"


def piece_count(s, k):
    return (ring_length(s, 1), 2, 1)[k]


def piece_length(s, k):
    return (ring_length(s, 2), ring_length(s, 2) // 2, 1)[k]


def reach(n, way, piece):
    return n // 2 if way == piece % 2 else n // 2 - 1


def hops(s, k):
    for piece in range(piece_count(s, k)):
        for way in (0, 1):
            for hop in range(1, reach(ring_length(s, k), way, piece) + 1):
                yield way, piece, hop


def plan():
    tasks = [("g", i) for i in range(5)]
    for s in range(len(STREAMS)):
        for k in range(3):
            if is_ring(s, k):
                tasks += [("l", s, k, piece) for piece in range(piece_count(s, k))]
                tasks += [("s", s, k, *which) for which in hops(s, k)]
            else:
                tasks.append(("d", s))
    link, arrive, done, order = {}, {}, {}, []

    def size(s, k):
        return piece_length(s, k) * UNITS[s] * 16 * 128 * 2

    def own(s, k, piece, off):
        if k == 0:
            at = {STREAMS[s][0]: off, STREAMS[s][1]: FAR_FIRST[ring_length(s, 1)][piece]}
            z_lo = at.get("z", 2) % 4
            return [("g", 0 if z_lo == 0 else 1 if at.get("x") == 2 else LATER[z_lo])]
        if k == 1:
            return [("l", s, 0, FAR_FIRST[ring_length(s, 1)].index(off))]
        return [("l", s, 1, 0), ("l", s, 1, 1)]

    def fresh(t):
        return t[0] == "s" and t[5] == reach(ring_length(t[1], t[2]), t[3], t[4])

    def filler(t):
        return fresh(t) and t[5] < ring_length(t[1], t[2]) // 2

    def ready(t):
        if t[0] == "g":
            return 0.0 if t[1] == 0 or ("g", t[1] - 1) in done else None
        came = []
        if t[0] == "d":
            need = own(t[1], 2, 0, 0)
        elif t[0] == "s":
            s, k, way, piece, hop = t[1:]
            n = ring_length(s, k)
            need = own(s, k, piece, hop if way == 0 else n - hop)
            came = [] if fresh(t) else [(s, k, way, piece, hop + 1)]
        else:
            s, k, piece = t[1:]
            need = own(s, k, piece, 0)
            came = [(s, k, way, piece, 1) for way in (0, 1)]
        if any(d not in done for d in need) or any(a not in arrive for a in came):
            return None
        at = max([done[d] for d in need] + [arrive[a] for a in came])
        if filler(t):
            at = max(at, link.get((STREAMS[t[1]][t[2]], t[3]), 0.0) - SLACK)
        return at

    def rank(t):
        if t[0] == "d":
            return (0,)
        if t[0] == "s":
            return (3 if filler(t) else 1, -t[2], -t[5], t[4])
        return (2, -t[2], t[3]) if t[0] == "l" else (4, t[1])

    now = 0.0
    while tasks:
        times = {t: ready(t) for t in tasks}
        able = [t for t in tasks if times[t] is not None and times[t] <= now + 1e-9]
        if not able:
            now = min(v for v in times.values() if v is not None)
            continue
        t = min(able, key=rank)
        tasks.remove(t)
        order.append(t)
        if t[0] == "g":
            now = max(now, PRODUCTS_FIRST) if t[1] == 0 else now + PRODUCTS_NEXT
        elif t[0] == "l":
            now += 3 * size(t[1], t[2]) / 4 / ADDS
        elif t[0] == "s":
            s, k, way, piece, hop = t[1:]
            now += 0.0 if fresh(t) else size(s, k) / 2 / ADDS
            key = (STREAMS[s][k], way)
            link[key] = max(now + 0.05, link.get(key, 0.0)) + 2 * size(s, k) / RATE
            arrive[t[1:]] = link[key] + LATE
        done[t] = now
    return order


def wait(ref, sem):
    pltpu.make_async_copy(ref, ref, sem).wait()


def remote(source, target, send_sem, recv_sem, device):
    return pltpu.make_async_remote_copy(
        src_ref=source,
        dst_ref=target,
        send_sem=send_sem,
        recv_sem=recv_sem,
        device_id=device,
        device_id_type=MESH_ID,
    )


class Sems:
    def __init__(self, ref):
        self.ref, self.used = ref, 0

    def take(self):
        self.used += 1
        return self.ref.at[self.used - 1]


class Ring:
    def __init__(self, s, k, me, place, view, landing, send_sem, sems):
        self.n, self.me, self.view, self.landing = ring_length(s, k), me, view, landing
        self.length, self.copies, self.came = piece_length(s, k), {}, {}
        self.near = [sems.take() for _ in range(piece_count(s, k))]
        slots = 2 * len(self.near)
        for way, piece, hop in hops(s, k):
            if hop == 1:
                slot, sem = 2 * piece + way, self.near[piece]
            else:
                slot, sem = slots, sems.take()
                slots += 1
            self.came[way, piece, hop] = landing.at[slot]
            self.copies[way, piece, hop] = remote(
                view(self.dest(way, hop), piece), landing.at[slot], send_sem, sem, place(self.dest(way, 1))
            )

    def dest(self, way, hop):
        return lax.rem(self.me + (hop if way == 0 else self.n - hop), self.n)

    def send(self, way, piece, hop):
        if hop < reach(self.n, way, piece):
            self.copies[way, piece, hop + 1].wait_recv()
            target, came = self.view(self.dest(way, hop), piece), self.came[way, piece, hop + 1]

            def add(i, _):
                target[i] = (target[i].astype(F32) + came[i].astype(F32)).astype(BF16)
                return 0

            lax.fori_loop(0, self.length, add, 0)
        self.copies[way, piece, hop].start()

    def arrive(self, piece):
        wait(self.landing.at[pl.ds(2 * piece, 2)], self.near[piece])
        return self.came[0, piece, 1], self.came[1, piece, 1]

    def last(self, piece):
        a, b = self.arrive(piece)
        target = self.view(self.me, piece)

        def add(i, _):
            total = target[i].astype(F32) + a[i].astype(F32)
            target[i] = (total + b[i].astype(F32)).astype(BF16)
            return 0

        lax.fori_loop(0, self.length, add, 0)


def kernel(normed, out_grads, out, lhs, rhs, *refs):
    many = len(STREAMS)
    partials = refs[:many]
    landings = [refs[many * (k + 1) : many * (k + 2)] for k in range(3)]
    squares, send_sem, recv_sem, load_sem, in_send, in_recv, fold_sem, heard = refs[many * 4 :]
    x, y, core = lax.axis_index("x"), lax.axis_index("y"), lax.axis_index("core")
    z_lo, z_hi = lax.axis_index("z_lo"), lax.axis_index("z_hi")
    place_of = {
        "x": lambda i: {"x": i},
        "y": lambda i: {"y": i},
        "z": lambda i: {"z_hi": i // 4, "z_lo": lax.rem(i, 4)},
    }
    here = {"x": x, "y": y, "z": z_hi * 4 + z_lo}
    other = 1 - core

    def columns(j, c):
        return pl.ds(pl.multiple_of((2 * j + c) * BLOCK, BLOCK), BLOCK)

    def block(group, i):
        if group == 0:
            return z_lo, lax.rem(x + 2 + i, 4)
        if group == 1:
            return lax.rem(z_lo + 1 + i, 4), lax.rem(x + 2, 4)
        off = next(o for o, g in LATER.items() if g == group)
        return lax.rem(z_lo + off, 4), lax.rem(x + 3 + i, 4)

    before = [sum(GROUPS[:group]) for group in range(len(GROUPS))]

    def own_load(group, i):
        zl, xj = block(group, i)
        return pltpu.make_async_copy(
            normed.at[:, columns(zl * 4 + xj, core)], lhs.at[before[group] + i, pl.ds(0, TOK)], load_sem.at[group]
        )

    def partner_send(group, i):
        zl, xj = block(group, i)
        return remote(
            normed.at[:, columns(zl * 4 + xj, other)],
            lhs.at[before[group] + i, pl.ds(TOK, TOK)],
            in_send.at[0],
            in_recv.at[before[group] + i],
            {"core": other},
        )

    blocks = [(group, i) for group, count in enumerate(GROUPS) for i in range(count)]
    grads_load = pltpu.make_async_copy(out_grads, rhs.at[pl.ds(0, TOK)], load_sem.at[len(GROUPS)])
    grads_send = remote(out_grads, rhs.at[pl.ds(TOK, TOK)], in_send.at[1], in_recv.at[16], {"core": other})

    barrier = pltpu.get_barrier_semaphore()
    neighbours = [{"core": other}]
    for axis in "xyz":
        for step in (1, LENGTH[axis] - 1):
            neighbours.append(place_of[axis](lax.rem(here[axis] + step, LENGTH[axis])))
    for device in neighbours:
        pl.semaphore_signal(barrier, inc=1, device_id=device, device_id_type=MESH_ID)
    grads_load.start()
    for where in blocks:
        own_load(*where).start()
    pl.semaphore_wait(barrier, len(neighbours))
    grads_send.start()
    for where in blocks:
        partner_send(*where).start()

    sems = Sems(recv_sem)
    firsts = [sum(UNITS[:s]) for s in range(len(STREAMS))]

    def tile(s, i):
        unit = firsts[s] + i
        return slice(unit // 8 * 16, unit // 8 * 16 + 16), slice(unit % 8 * 128, unit % 8 * 128 + 128)

    def views(s):
        ref = partials[s]
        a1, a2, a3 = STREAMS[s]
        n2, n3 = LENGTH[a2], LENGTH[a3]
        mine = here[a1] * n2 * n3

        def first(dest, piece):
            i2 = lax.rem(here[a2] + FAR_FIRST[n2][piece], n2)
            return ref.at[pl.ds(dest * n2 * n3 + n3 * i2, n3)]

        def second(dest, piece):
            return ref.at[pl.ds(mine + n3 * dest + n3 // 2 * piece, n3 // 2)]

        def third(dest, piece=0):
            return ref.at[pl.ds(mine + n3 * here[a2] + dest, 1)]

        return first, second, third

    stages, directs = {}, {}
    for s in range(len(STREAMS)):
        for k in range(3):
            axis, view, landing = STREAMS[s][k], views(s)[k], landings[k][s]
            if is_ring(s, k):
                stages[s, k] = Ring(s, k, here[axis], place_of[axis], view, landing, send_sem.at[s], sems)
            else:
                directs[s] = sems.take()

    grads_load.wait()
    grads_send.wait_recv()

    def products(group):
        first = before[group]
        wait(lhs.at[pl.ds(first, GROUPS[group]), pl.ds(0, TOK)], load_sem.at[group])

        def body(i, _):
            partner_send(group, i).wait_recv()
            zl, xj = block(group, i)
            total = lax.dot_general(
                lhs[first + i], rhs[...], (((0,), (0,)), ((), ())), preferred_element_type=F32
            ).astype(BF16)
            for yi in range(4):
                for zh in range(2):
                    at = {"x": xj, "y": yi, "z": zh * 4 + zl}
                    rows = total[(yi * 2 + zh) * ROWS : (yi * 2 + zh + 1) * ROWS]
                    for s, (a1, a2, a3) in enumerate(STREAMS):
                        for u in range(UNITS[s]):
                            place = (at[a1] * LENGTH[a2] + at[a2]) * LENGTH[a3] + at[a3]
                            partials[s][place, u * 16 : u * 16 + 16] = rows[tile(s, u)]
            return 0

        lax.fori_loop(0, GROUPS[group], body, 0)

    sums = jnp.zeros((8, 128), F32)

    def finish(s, total, sums):
        for u in range(UNITS[s]):
            part = total[u * 16 : u * 16 + 16]
            out[tile(s, u)] = part
            sums = sums + part[:8] * part[:8] + part[8:] * part[8:]
        return sums

    order = plan()
    rounds = [t for t in order if t[0] == "l" and t[2] == 0 and STREAMS[t[1]][0] == "z"]
    for t in order:
        if t[0] == "g":
            products(t[1])
        elif t[0] == "d":
            s, axis = t[1], STREAMS[t[1]][2]
            for off in FAR_FIRST[LENGTH[axis]][:-1]:
                dest = lax.rem(here[axis] + off, LENGTH[axis])
                landing = landings[2][s].at[off - 1]
                remote(views(s)[2](dest), landing, send_sem.at[s], directs[s], place_of[axis](dest)).start()
        elif t[0] == "s":
            stages[t[1], t[2]].send(*t[3:])
        elif t[2] < 2:
            stages[t[1], t[2]].last(t[3])
        else:
            ring = stages[t[1], 2]
            a, b = ring.arrive(0)
            total = ring.view(ring.me, 0)[0].astype(F32) + a[0].astype(F32)
            sums = finish(t[1], total + b[0].astype(F32), sums)
        if t == rounds[-1]:
            pl.semaphore_signal(heard, inc=1, device_id={"core": other}, device_id_type=MESH_ID)
    for s, sem in directs.items():
        wait(landings[2][s], sem)
        total = views(s)[2](here[STREAMS[s][2]])[0].astype(F32)
        for i in range(LENGTH[STREAMS[s][2]] - 1):
            total = total + landings[2][s][i, 0].astype(F32)
        sums = finish(s, total, sums)
    pl.semaphore_wait(heard, 1)

    def fold(turn, part, offsets, place):
        box = squares.at[turn]
        box[0:1] = part
        for i, off in enumerate(offsets):
            target = box.at[pl.ds(i + 1, 1)]
            remote(box.at[pl.ds(0, 1)], target, fold_sem.at[turn, 0], fold_sem.at[turn, 1], place(off)).start()
        wait(box.at[pl.ds(1, len(offsets))], fold_sem.at[turn, 1])
        return jnp.sum(box[...], axis=0, keepdims=True)

    def along_z(off):
        return {**place_of["z"](lax.rem(here["z"] + off[1], 8)), "core": lax.rem(core + off[0], 2)}

    def across(off):
        return {"x": lax.rem(x + off[0], 4), "y": lax.rem(y + off[1], 4)}

    part = jnp.sum(sums, axis=0, keepdims=True)
    part = fold(0, part, [(c, i) for i in FAR_FIRST[8] for c in (1, 0)][:-1], along_z)
    part = fold(1, part, [(i, k) for i in FAR_FIRST[4] for k in FAR_FIRST[4]][:-1], across)
    total = jnp.sum(part, axis=1, keepdims=True)
    limit = jnp.sqrt(jnp.full((1, 1), float(D * C), F32))
    clip = jnp.minimum(1.0, limit / (jnp.sqrt(total) + 1e-06))
    out[...] = out[...] * clip

    for s, partial in enumerate(partials):
        wait(partial.at[pl.ds(0, 127)], send_sem.at[s])
    for turn in (0, 1):
        wait(squares.at[turn, pl.ds(1, 15)], fold_sem.at[turn, 0])
    wait(lhs.at[:, pl.ds(0, TOK)], in_send.at[0])
    wait(rhs.at[pl.ds(0, TOK)], in_send.at[1])


def scaled_gradient(normed, out_grads):
    landings, sems, many = [], 0, len(STREAMS)
    partials = [pltpu.VMEM((128, units * 16, 128), BF16) for units in UNITS]
    for k in range(3):
        for s in range(many):
            tail = (piece_length(s, k), UNITS[s] * 16, 128)
            if is_ring(s, k):
                slots = len(list(hops(s, k)))
                sems += slots - piece_count(s, k)
            else:
                slots = ring_length(s, k) - 1
                sems += 1
            landings.append(pltpu.VMEM((slots, *tail), BF16))
    return pl.pallas_call(
        kernel,
        out_shape=pltpu.VMEM((ROWS, C), F32),
        in_specs=[pl.BlockSpec(memory_space=pl.ANY)] * 2,
        out_specs=pl.BlockSpec(memory_space=pltpu.VMEM),
        scratch_shapes=[
            pltpu.VMEM((16, 2 * TOK, BLOCK), BF16),
            pltpu.VMEM((2 * TOK, C), BF16),
            *partials,
            *landings,
            pltpu.VMEM((2, 16, 128), F32),
            pltpu.SemaphoreType.DMA((many,)),
            pltpu.SemaphoreType.DMA((sems,)),
            pltpu.SemaphoreType.DMA((len(GROUPS) + 1,)),
            pltpu.SemaphoreType.DMA((2,)),
            pltpu.SemaphoreType.DMA((17,)),
            pltpu.SemaphoreType.DMA((2, 2)),
            pltpu.SemaphoreType.REGULAR,
        ],
        compiler_params=pltpu.CompilerParams(collective_id=0, has_side_effects=True),
    )(normed, out_grads)


def shards(normed, out_grads, weight, moment, variance):
    scaled = scaled_gradient(normed, out_grads)
    new_moment = 0.9 * moment + 0.1 * scaled
    new_variance = 0.95 * variance + 0.05 * scaled * scaled
    first = new_moment / (1.0 - 0.9**STEP)
    second = new_variance / (1.0 - 0.95**STEP)
    new_weight = weight - 0.01 * (first / (jnp.sqrt(second) + 1e-08) + 0.1 * weight)
    return (new_weight, new_moment, new_variance)


def solution(mesh):
    split = Mesh(mesh.devices.reshape(SIZES), AXES)
    spec = P(AXES, None)
    return jax.shard_map(
        shards, mesh=split, in_specs=(spec,) * 5, out_specs=(spec,) * 3, check_vma=False
    )
```

```python
import jax
import jax.numpy as jnp
from jax import lax
from jax.experimental import pallas as pl
from jax.experimental.pallas import tpu as pltpu
from jax.sharding import Mesh
from jax.sharding import PartitionSpec as P

STEP = 10
AXES = ("z_lo", "x", "core", "y", "z_hi")
SIZES = (4, 4, 2, 4, 2)
MESH_ID = pl.DeviceIdType.MESH
F32, BF16 = jnp.float32, jnp.bfloat16
D, C, TOK, BLOCK, ROWS = 8192, 1024, 256, 256, 32

STREAMS = ("xzy", "yzx", "zxy")
UNITS = (6, 6, 4)
LENGTH = {"x": 4, "y": 4, "z": 8}
FAR_FIRST = {4: (2, 3, 1, 0), 8: (4, 5, 3, 6, 2, 7, 1, 0)}
BLOCKS = (
    *((0, 2), (0, 3), (0, 1), (0, 0), (1, 2), (3, 3), (1, 1), (3, 0)),
    *((3, 2), (3, 1), (1, 3), (1, 0), (2, 2), (2, 3), (2, 1), (2, 0)),
)
PRODUCTS_FIRST, PRODUCTS_NEXT, RATE, LATE, ADDS, SLACK = 5.1, 0.47, 93.6e3, 2.0, 0.9e6, 3.0


def ring_length(s, k):
    return LENGTH[STREAMS[s][k]]


def is_ring(s, k):
    return k < 2 or STREAMS[s][2] == "z"


def piece_count(s, k):
    return (ring_length(s, 1), 2, 1)[k]


def piece_length(s, k):
    return (ring_length(s, 2), ring_length(s, 2) // 2, 1)[k]


def reach(n, way, piece):
    return n // 2 if way == piece % 2 else n // 2 - 1


def hops(s, k):
    for piece in range(piece_count(s, k)):
        for way in (0, 1):
            for hop in range(1, reach(ring_length(s, k), way, piece) + 1):
                yield way, piece, hop


def plan():
    tasks = [("g", i) for i in range(16)]
    for s in range(len(STREAMS)):
        for k in range(3):
            if is_ring(s, k):
                tasks += [("l", s, k, piece) for piece in range(piece_count(s, k))]
                tasks += [("s", s, k, *which) for which in hops(s, k)]
            else:
                tasks.append(("d", s))
    link, arrive, done, order = {}, {}, {}, []

    def size(s, k):
        return piece_length(s, k) * UNITS[s] * 16 * 128 * 2

    def own(s, k, piece, off):
        if k == 0:
            at = {STREAMS[s][0]: off, STREAMS[s][1]: FAR_FIRST[ring_length(s, 1)][piece]}
            z_los = [at["z"] % 4] if "z" in at else range(4)
            xs = [at["x"]] if "x" in at else range(4)
            return [("g", max(BLOCKS.index((z_lo, x)) for z_lo in z_los for x in xs))]
        if k == 1:
            return [("l", s, 0, FAR_FIRST[ring_length(s, 1)].index(off))]
        return [("l", s, 1, 0), ("l", s, 1, 1)]

    def fresh(t):
        return t[0] == "s" and t[5] == reach(ring_length(t[1], t[2]), t[3], t[4])

    def filler(t):
        return fresh(t) and t[5] < ring_length(t[1], t[2]) // 2

    def ready(t):
        if t[0] == "g":
            return 0.0 if t[1] == 0 or ("g", t[1] - 1) in done else None
        came = []
        if t[0] == "d":
            need = own(t[1], 2, 0, 0)
        elif t[0] == "s":
            s, k, way, piece, hop = t[1:]
            n = ring_length(s, k)
            need = own(s, k, piece, hop if way == 0 else n - hop)
            came = [] if fresh(t) else [(s, k, way, piece, hop + 1)]
        else:
            s, k, piece = t[1:]
            need = own(s, k, piece, 0)
            came = [(s, k, way, piece, 1) for way in (0, 1)]
        if any(d not in done for d in need) or any(a not in arrive for a in came):
            return None
        at = max([done[d] for d in need] + [arrive[a] for a in came])
        if filler(t):
            at = max(at, link.get((STREAMS[t[1]][t[2]], t[3]), 0.0) - SLACK)
        return at

    def rank(t):
        if t[0] == "d":
            return (0,)
        if t[0] == "s":
            return (3 if filler(t) else 1, -t[2], -t[5], t[4])
        return (2, -t[2], t[3]) if t[0] == "l" else (4, t[1])

    now = 0.0
    while tasks:
        times = {t: ready(t) for t in tasks}
        able = [t for t in tasks if times[t] is not None and times[t] <= now + 1e-9]
        if not able:
            now = min(v for v in times.values() if v is not None)
            continue
        t = min(able, key=rank)
        tasks.remove(t)
        order.append(t)
        if t[0] == "g":
            now = max(now, PRODUCTS_FIRST) if t[1] == 0 else now + PRODUCTS_NEXT
        elif t[0] == "l":
            now += 3 * size(t[1], t[2]) / 4 / ADDS
        elif t[0] == "s":
            s, k, way, piece, hop = t[1:]
            now += 0.0 if fresh(t) else size(s, k) / 2 / ADDS
            key = (STREAMS[s][k], way)
            link[key] = max(now + 0.05, link.get(key, 0.0)) + 2 * size(s, k) / RATE
            arrive[t[1:]] = link[key] + LATE
        done[t] = now
    return order


def wait(ref, sem):
    pltpu.make_async_copy(ref, ref, sem).wait()


def remote(source, target, send_sem, recv_sem, device):
    return pltpu.make_async_remote_copy(
        src_ref=source,
        dst_ref=target,
        send_sem=send_sem,
        recv_sem=recv_sem,
        device_id=device,
        device_id_type=MESH_ID,
    )


class Sems:
    def __init__(self, ref):
        self.ref, self.used = ref, 0

    def take(self):
        self.used += 1
        return self.ref.at[self.used - 1]


class Ring:
    def __init__(self, s, k, me, place, view, landing, send_sem, sems):
        self.n, self.me, self.view, self.landing = ring_length(s, k), me, view, landing
        self.length, self.copies, self.came = piece_length(s, k), {}, {}
        self.near = [sems.take() for _ in range(piece_count(s, k))]
        slots = 2 * len(self.near)
        for way, piece, hop in hops(s, k):
            if hop == 1:
                slot, sem = 2 * piece + way, self.near[piece]
            else:
                slot, sem = slots, sems.take()
                slots += 1
            self.came[way, piece, hop] = landing.at[slot]
            self.copies[way, piece, hop] = remote(
                view(self.dest(way, hop), piece), landing.at[slot], send_sem, sem, place(self.dest(way, 1))
            )

    def dest(self, way, hop):
        return lax.rem(self.me + (hop if way == 0 else self.n - hop), self.n)

    def send(self, way, piece, hop):
        if hop < reach(self.n, way, piece):
            self.copies[way, piece, hop + 1].wait_recv()
            target, came = self.view(self.dest(way, hop), piece), self.came[way, piece, hop + 1]

            def add(i, _):
                target[i] = (target[i].astype(F32) + came[i].astype(F32)).astype(BF16)
                return 0

            lax.fori_loop(0, self.length, add, 0)
        self.copies[way, piece, hop].start()

    def arrive(self, piece):
        wait(self.landing.at[pl.ds(2 * piece, 2)], self.near[piece])
        return self.came[0, piece, 1], self.came[1, piece, 1]

    def last(self, piece):
        a, b = self.arrive(piece)
        target = self.view(self.me, piece)

        def add(i, _):
            total = target[i].astype(F32) + a[i].astype(F32)
            target[i] = (total + b[i].astype(F32)).astype(BF16)
            return 0

        lax.fori_loop(0, self.length, add, 0)


def kernel(normed, out_grads, out, lhs, rhs, *refs):
    many = len(STREAMS)
    partials = refs[:many]
    landings = [refs[many * (k + 1) : many * (k + 2)] for k in range(3)]
    squares, send_sem, recv_sem, load_sem, in_send, in_recv, fold_sem, heard = refs[many * 4 :]
    x, y, core = lax.axis_index("x"), lax.axis_index("y"), lax.axis_index("core")
    z_lo, z_hi = lax.axis_index("z_lo"), lax.axis_index("z_hi")
    place_of = {
        "x": lambda i: {"x": i},
        "y": lambda i: {"y": i},
        "z": lambda i: {"z_hi": i // 4, "z_lo": lax.rem(i, 4)},
    }
    here = {"x": x, "y": y, "z": z_hi * 4 + z_lo}
    other = 1 - core

    def columns(j, c):
        return pl.ds(pl.multiple_of((2 * j + c) * BLOCK, BLOCK), BLOCK)

    def block(pos):
        return lax.rem(z_lo + BLOCKS[pos][0], 4), lax.rem(x + BLOCKS[pos][1], 4)

    def own_load(pos):
        zl, xj = block(pos)
        return pltpu.make_async_copy(
            normed.at[:, columns(zl * 4 + xj, core)], lhs.at[pos, pl.ds(0, TOK)], load_sem.at[pos // 4]
        )

    def partner_send(pos):
        zl, xj = block(pos)
        return remote(
            normed.at[:, columns(zl * 4 + xj, other)],
            lhs.at[pos, pl.ds(TOK, TOK)],
            in_send.at[0],
            in_recv.at[pos],
            {"core": other},
        )

    grads_load = pltpu.make_async_copy(out_grads, rhs.at[pl.ds(0, TOK)], load_sem.at[4])
    grads_send = remote(out_grads, rhs.at[pl.ds(TOK, TOK)], in_send.at[1], in_recv.at[16], {"core": other})

    barrier = pltpu.get_barrier_semaphore()
    neighbours = [{"core": other}]
    for axis in "xyz":
        for step in (1, LENGTH[axis] - 1):
            neighbours.append(place_of[axis](lax.rem(here[axis] + step, LENGTH[axis])))
    for device in neighbours:
        pl.semaphore_signal(barrier, inc=1, device_id=device, device_id_type=MESH_ID)
    grads_load.start()
    for pos in range(16):
        own_load(pos).start()
    pl.semaphore_wait(barrier, len(neighbours))
    grads_send.start()
    for pos in range(16):
        partner_send(pos).start()

    sems = Sems(recv_sem)
    firsts = [sum(UNITS[:s]) for s in range(len(STREAMS))]

    def tile(s, i):
        unit = firsts[s] + i
        return slice(unit // 8 * 16, unit // 8 * 16 + 16), slice(unit % 8 * 128, unit % 8 * 128 + 128)

    def views(s):
        ref = partials[s]
        a1, a2, a3 = STREAMS[s]
        n2, n3 = LENGTH[a2], LENGTH[a3]
        mine = here[a1] * n2 * n3

        def first(dest, piece):
            i2 = lax.rem(here[a2] + FAR_FIRST[n2][piece], n2)
            return ref.at[pl.ds(dest * n2 * n3 + n3 * i2, n3)]

        def second(dest, piece):
            return ref.at[pl.ds(mine + n3 * dest + n3 // 2 * piece, n3 // 2)]

        def third(dest, piece=0):
            return ref.at[pl.ds(mine + n3 * here[a2] + dest, 1)]

        return first, second, third

    stages, directs = {}, {}
    for s in range(len(STREAMS)):
        for k in range(3):
            axis, view, landing = STREAMS[s][k], views(s)[k], landings[k][s]
            if is_ring(s, k):
                stages[s, k] = Ring(s, k, here[axis], place_of[axis], view, landing, send_sem.at[s], sems)
            else:
                directs[s] = sems.take()

    grads_load.wait()
    grads_send.wait_recv()

    def product(pos):
        if pos % 4 == 0:
            wait(lhs.at[pl.ds(pos, 4), pl.ds(0, TOK)], load_sem.at[pos // 4])
        partner_send(pos).wait_recv()
        zl, xj = block(pos)
        total = lax.dot_general(
            lhs[pos], rhs[...], (((0,), (0,)), ((), ())), preferred_element_type=F32
        ).astype(BF16)
        for yi in range(4):
            for zh in range(2):
                at = {"x": xj, "y": yi, "z": zh * 4 + zl}
                rows = total[(yi * 2 + zh) * ROWS : (yi * 2 + zh + 1) * ROWS]
                for s, (a1, a2, a3) in enumerate(STREAMS):
                    for u in range(UNITS[s]):
                        place = (at[a1] * LENGTH[a2] + at[a2]) * LENGTH[a3] + at[a3]
                        partials[s][place, u * 16 : u * 16 + 16] = rows[tile(s, u)]

    sums = jnp.zeros((8, 128), F32)

    def finish(s, total, sums):
        for u in range(UNITS[s]):
            part = total[u * 16 : u * 16 + 16]
            out[tile(s, u)] = part
            sums = sums + part[:8] * part[:8] + part[8:] * part[8:]
        return sums

    order = plan()
    rounds = [t for t in order if t[0] == "l" and t[2] == 0 and STREAMS[t[1]][0] == "z"]
    for t in order:
        if t[0] == "g":
            product(t[1])
        elif t[0] == "d":
            s, axis = t[1], STREAMS[t[1]][2]
            for off in FAR_FIRST[LENGTH[axis]][:-1]:
                dest = lax.rem(here[axis] + off, LENGTH[axis])
                landing = landings[2][s].at[off - 1]
                remote(views(s)[2](dest), landing, send_sem.at[s], directs[s], place_of[axis](dest)).start()
        elif t[0] == "s":
            stages[t[1], t[2]].send(*t[3:])
        elif t[2] < 2:
            stages[t[1], t[2]].last(t[3])
        else:
            ring = stages[t[1], 2]
            a, b = ring.arrive(0)
            total = ring.view(ring.me, 0)[0].astype(F32) + a[0].astype(F32)
            sums = finish(t[1], total + b[0].astype(F32), sums)
        if t == rounds[-1]:
            pl.semaphore_signal(heard, inc=1, device_id={"core": other}, device_id_type=MESH_ID)
    for s, sem in directs.items():
        wait(landings[2][s], sem)
        total = views(s)[2](here[STREAMS[s][2]])[0].astype(F32)
        for i in range(LENGTH[STREAMS[s][2]] - 1):
            total = total + landings[2][s][i, 0].astype(F32)
        sums = finish(s, total, sums)
    pl.semaphore_wait(heard, 1)

    def fold(turn, part, offsets, place):
        box = squares.at[turn]
        box[0:1] = part
        for i, off in enumerate(offsets):
            target = box.at[pl.ds(i + 1, 1)]
            remote(box.at[pl.ds(0, 1)], target, fold_sem.at[turn, 0], fold_sem.at[turn, 1], place(off)).start()
        wait(box.at[pl.ds(1, len(offsets))], fold_sem.at[turn, 1])
        return jnp.sum(box[...], axis=0, keepdims=True)

    def along_z(off):
        return {**place_of["z"](lax.rem(here["z"] + off[1], 8)), "core": lax.rem(core + off[0], 2)}

    def across(off):
        return {"x": lax.rem(x + off[0], 4), "y": lax.rem(y + off[1], 4)}

    part = jnp.sum(sums, axis=0, keepdims=True)
    part = fold(0, part, [(c, i) for i in FAR_FIRST[8] for c in (1, 0)][:-1], along_z)
    part = fold(1, part, [(i, k) for i in FAR_FIRST[4] for k in FAR_FIRST[4]][:-1], across)
    total = jnp.sum(part, axis=1, keepdims=True)
    limit = jnp.sqrt(jnp.full((1, 1), float(D * C), F32))
    clip = jnp.minimum(1.0, limit / (jnp.sqrt(total) + 1e-06))
    out[...] = out[...] * clip

    for s, partial in enumerate(partials):
        wait(partial.at[pl.ds(0, 127)], send_sem.at[s])
    for turn in (0, 1):
        wait(squares.at[turn, pl.ds(1, 15)], fold_sem.at[turn, 0])
    wait(lhs.at[:, pl.ds(0, TOK)], in_send.at[0])
    wait(rhs.at[pl.ds(0, TOK)], in_send.at[1])


def scaled_gradient(normed, out_grads):
    landings, sems, many = [], 0, len(STREAMS)
    partials = [pltpu.VMEM((128, units * 16, 128), BF16) for units in UNITS]
    for k in range(3):
        for s in range(many):
            tail = (piece_length(s, k), UNITS[s] * 16, 128)
            if is_ring(s, k):
                slots = len(list(hops(s, k)))
                sems += slots - piece_count(s, k)
            else:
                slots = ring_length(s, k) - 1
                sems += 1
            landings.append(pltpu.VMEM((slots, *tail), BF16))
    return pl.pallas_call(
        kernel,
        out_shape=pltpu.VMEM((ROWS, C), F32),
        in_specs=[pl.BlockSpec(memory_space=pl.ANY)] * 2,
        out_specs=pl.BlockSpec(memory_space=pltpu.VMEM),
        scratch_shapes=[
            pltpu.VMEM((16, 2 * TOK, BLOCK), BF16),
            pltpu.VMEM((2 * TOK, C), BF16),
            *partials,
            *landings,
            pltpu.VMEM((2, 16, 128), F32),
            pltpu.SemaphoreType.DMA((many,)),
            pltpu.SemaphoreType.DMA((sems,)),
            pltpu.SemaphoreType.DMA((5,)),
            pltpu.SemaphoreType.DMA((2,)),
            pltpu.SemaphoreType.DMA((17,)),
            pltpu.SemaphoreType.DMA((2, 2)),
            pltpu.SemaphoreType.REGULAR,
        ],
        compiler_params=pltpu.CompilerParams(collective_id=0, has_side_effects=True),
    )(normed, out_grads)


def shards(normed, out_grads, weight, moment, variance):
    scaled = scaled_gradient(normed, out_grads)
    new_moment = 0.9 * moment + 0.1 * scaled
    new_variance = 0.95 * variance + 0.05 * scaled * scaled
    first = new_moment / (1.0 - 0.9**STEP)
    second = new_variance / (1.0 - 0.95**STEP)
    new_weight = weight - 0.01 * (first / (jnp.sqrt(second) + 1e-08) + 0.1 * weight)
    return (new_weight, new_moment, new_variance)


def solution(mesh):
    split = Mesh(mesh.devices.reshape(SIZES), AXES)
    spec = P(AXES, None)
    return jax.shard_map(
        shards, mesh=split, in_specs=(spec,) * 5, out_specs=(spec,) * 3, check_vma=False
    )
```

```python
import jax
import jax.numpy as jnp
from jax import lax
from jax.experimental import pallas as pl
from jax.experimental.pallas import tpu as pltpu
from jax.sharding import Mesh
from jax.sharding import PartitionSpec as P

STEP = 10
AXES = ("z_lo", "x", "core", "y", "z_hi")
SIZES = (4, 4, 2, 4, 2)
MESH_ID = pl.DeviceIdType.MESH
F32, BF16 = jnp.float32, jnp.bfloat16
D, C, TOK, BLOCK, ROWS = 8192, 1024, 256, 256, 32

STREAMS = ("xzy", "yzx", "zxy")
UNITS = (6, 6, 4)
LENGTH = {"x": 4, "y": 4, "z": 8}
FAR_FIRST = {4: (2, 3, 1, 0), 8: (4, 5, 3, 6, 2, 7, 1, 0)}
BLOCKS = (
    *((0, 2), (0, 3), (0, 1), (0, 0), (1, 2), (3, 3), (1, 1), (3, 0)),
    *((3, 2), (3, 1), (1, 3), (1, 0), (2, 2), (2, 3), (2, 1), (2, 0)),
)
PRODUCTS_FIRST, PRODUCTS_NEXT, RATE, LATE, ADDS, SLACK = 5.1, 0.47, 93.6e3, 1.6, 0.9e6, 3.0


def ring_length(s, k):
    return LENGTH[STREAMS[s][k]]


def is_ring(s, k):
    return k < 2 or STREAMS[s][2] == "z"


def piece_count(s, k):
    return (ring_length(s, 1), 2, 1)[k]


def piece_length(s, k):
    return (ring_length(s, 2), ring_length(s, 2) // 2, 1)[k]


def reach(n, way, piece):
    return n // 2 if way == piece % 2 else n // 2 - 1


def hops(s, k):
    for piece in range(piece_count(s, k)):
        for way in (0, 1):
            for hop in range(1, reach(ring_length(s, k), way, piece) + 1):
                yield way, piece, hop


def plan():
    tasks = [("g", i) for i in range(16)]
    for s in range(len(STREAMS)):
        for k in range(3):
            if is_ring(s, k):
                tasks += [("l", s, k, piece) for piece in range(piece_count(s, k))]
                tasks += [("s", s, k, *which) for which in hops(s, k)]
            else:
                tasks += [("d", s, 0), ("d", s, 1)]
    link, arrive, done, order = {}, {}, {}, []

    def size(s, k):
        return piece_length(s, k) * UNITS[s] * 16 * 128 * 2

    def own(s, k, piece, off):
        if k == 0:
            at = {STREAMS[s][0]: off, STREAMS[s][1]: FAR_FIRST[ring_length(s, 1)][piece]}
            z_los = [at["z"] % 4] if "z" in at else range(4)
            xs = [at["x"]] if "x" in at else range(4)
            return [("g", max(BLOCKS.index((z_lo, x)) for z_lo in z_los for x in xs))]
        if k == 1:
            return [("l", s, 0, FAR_FIRST[ring_length(s, 1)].index(off))]
        return [("l", s, 1, 0), ("l", s, 1, 1)]

    def fresh(t):
        return t[0] == "s" and t[5] == reach(ring_length(t[1], t[2]), t[3], t[4])

    def filler(t):
        return fresh(t) and t[5] < ring_length(t[1], t[2]) // 2

    def ready(t):
        if t[0] == "g":
            return 0.0 if t[1] == 0 or ("g", t[1] - 1) in done else None
        came = []
        if t[0] == "d":
            need = [("l", t[1], 1, t[2])]
        elif t[0] == "s":
            s, k, way, piece, hop = t[1:]
            n = ring_length(s, k)
            need = own(s, k, piece, hop if way == 0 else n - hop)
            came = [] if fresh(t) else [(s, k, way, piece, hop + 1)]
        else:
            s, k, piece = t[1:]
            need = own(s, k, piece, 0)
            came = [(s, k, way, piece, 1) for way in (0, 1)]
        if any(d not in done for d in need) or any(a not in arrive for a in came):
            return None
        at = max([done[d] for d in need] + [arrive[a] for a in came])
        if filler(t):
            at = max(at, link.get((STREAMS[t[1]][t[2]], t[3]), 0.0) - SLACK)
        return at

    def rank(t):
        if t[0] == "d":
            return (0,)
        if t[0] == "s":
            return (3 if filler(t) else 1, -t[2], -t[5], t[4])
        return (2, -t[2], t[3]) if t[0] == "l" else (4, t[1])

    now = 0.0
    while tasks:
        times = {t: ready(t) for t in tasks}
        able = [t for t in tasks if times[t] is not None and times[t] <= now + 1e-9]
        if not able:
            now = min(v for v in times.values() if v is not None)
            continue
        t = min(able, key=rank)
        tasks.remove(t)
        order.append(t)
        if t[0] == "g":
            now = max(now, PRODUCTS_FIRST) if t[1] == 0 else now + PRODUCTS_NEXT
        elif t[0] == "l":
            now += 3 * size(t[1], t[2]) / 4 / ADDS
        elif t[0] == "s":
            s, k, way, piece, hop = t[1:]
            now += 0.0 if fresh(t) else size(s, k) / 2 / ADDS
            key = (STREAMS[s][k], way)
            link[key] = max(now + 0.05, link.get(key, 0.0)) + 2 * size(s, k) / RATE
            arrive[t[1:]] = link[key] + LATE
        done[t] = now
    return order


def wait(ref, sem):
    pltpu.make_async_copy(ref, ref, sem).wait()


def remote(source, target, send_sem, recv_sem, device):
    return pltpu.make_async_remote_copy(
        src_ref=source,
        dst_ref=target,
        send_sem=send_sem,
        recv_sem=recv_sem,
        device_id=device,
        device_id_type=MESH_ID,
    )


class Sems:
    def __init__(self, ref):
        self.ref, self.used = ref, 0

    def take(self):
        self.used += 1
        return self.ref.at[self.used - 1]


class Ring:
    def __init__(self, s, k, me, place, view, landing, send_sem, sems):
        self.n, self.me, self.view, self.landing = ring_length(s, k), me, view, landing
        self.length, self.copies, self.came = piece_length(s, k), {}, {}
        self.near = [sems.take() for _ in range(piece_count(s, k))]
        slots = 2 * len(self.near)
        for way, piece, hop in hops(s, k):
            if hop == 1:
                slot, sem = 2 * piece + way, self.near[piece]
            else:
                slot, sem = slots, sems.take()
                slots += 1
            self.came[way, piece, hop] = landing.at[slot]
            self.copies[way, piece, hop] = remote(
                view(self.dest(way, hop), piece), landing.at[slot], send_sem, sem, place(self.dest(way, 1))
            )

    def dest(self, way, hop):
        return lax.rem(self.me + (hop if way == 0 else self.n - hop), self.n)

    def send(self, way, piece, hop):
        if hop < reach(self.n, way, piece):
            self.copies[way, piece, hop + 1].wait_recv()
            target, came = self.view(self.dest(way, hop), piece), self.came[way, piece, hop + 1]

            def add(i, _):
                target[i] = (target[i].astype(F32) + came[i].astype(F32)).astype(BF16)
                return 0

            lax.fori_loop(0, self.length, add, 0)
        self.copies[way, piece, hop].start()

    def arrive(self, piece):
        wait(self.landing.at[pl.ds(2 * piece, 2)], self.near[piece])
        return self.came[0, piece, 1], self.came[1, piece, 1]

    def last(self, piece):
        a, b = self.arrive(piece)
        target = self.view(self.me, piece)

        def add(i, _):
            total = target[i].astype(F32) + a[i].astype(F32)
            target[i] = (total + b[i].astype(F32)).astype(BF16)
            return 0

        lax.fori_loop(0, self.length, add, 0)


def kernel(normed, out_grads, out, lhs, rhs, *refs):
    many = len(STREAMS)
    partials = refs[:many]
    landings = [refs[many * (k + 1) : many * (k + 2)] for k in range(3)]
    squares, send_sem, recv_sem, load_sem, in_send, in_recv, fold_sem, heard = refs[many * 4 :]
    x, y, core = lax.axis_index("x"), lax.axis_index("y"), lax.axis_index("core")
    z_lo, z_hi = lax.axis_index("z_lo"), lax.axis_index("z_hi")
    place_of = {
        "x": lambda i: {"x": i},
        "y": lambda i: {"y": i},
        "z": lambda i: {"z_hi": i // 4, "z_lo": lax.rem(i, 4)},
    }
    here = {"x": x, "y": y, "z": z_hi * 4 + z_lo}
    other = 1 - core

    def columns(j, c):
        return pl.ds(pl.multiple_of((2 * j + c) * BLOCK, BLOCK), BLOCK)

    def block(pos):
        return lax.rem(z_lo + BLOCKS[pos][0], 4), lax.rem(x + BLOCKS[pos][1], 4)

    def own_load(pos):
        zl, xj = block(pos)
        return pltpu.make_async_copy(
            normed.at[:, columns(zl * 4 + xj, core)], lhs.at[pos, pl.ds(0, TOK)], load_sem.at[pos // 4]
        )

    def partner_send(pos):
        zl, xj = block(pos)
        return remote(
            normed.at[:, columns(zl * 4 + xj, other)],
            lhs.at[pos, pl.ds(TOK, TOK)],
            in_send.at[0],
            in_recv.at[pos],
            {"core": other},
        )

    grads_load = pltpu.make_async_copy(out_grads, rhs.at[pl.ds(0, TOK)], load_sem.at[4])
    grads_send = remote(out_grads, rhs.at[pl.ds(TOK, TOK)], in_send.at[1], in_recv.at[16], {"core": other})

    barrier = pltpu.get_barrier_semaphore()
    neighbours = [{"core": other}]
    for axis in "xyz":
        for step in (1, LENGTH[axis] - 1):
            neighbours.append(place_of[axis](lax.rem(here[axis] + step, LENGTH[axis])))
    for device in neighbours:
        pl.semaphore_signal(barrier, inc=1, device_id=device, device_id_type=MESH_ID)
    grads_load.start()
    for pos in range(16):
        own_load(pos).start()
    pl.semaphore_wait(barrier, len(neighbours))
    grads_send.start()
    for pos in range(16):
        partner_send(pos).start()

    sems = Sems(recv_sem)
    firsts = [sum(UNITS[:s]) for s in range(len(STREAMS))]

    def tile(s, i):
        unit = firsts[s] + i
        return slice(unit // 8 * 16, unit // 8 * 16 + 16), slice(unit % 8 * 128, unit % 8 * 128 + 128)

    def views(s):
        ref = partials[s]
        a1, a2, a3 = STREAMS[s]
        n2, n3 = LENGTH[a2], LENGTH[a3]
        mine = here[a1] * n2 * n3

        def first(dest, piece):
            i2 = lax.rem(here[a2] + FAR_FIRST[n2][piece], n2)
            return ref.at[pl.ds(dest * n2 * n3 + n3 * i2, n3)]

        def second(dest, piece):
            half = lax.rem(here[a3] // (n3 // 2) + 1 + piece, 2)
            return ref.at[pl.ds(mine + n3 * dest + n3 // 2 * half, n3 // 2)]

        def third(dest, piece=0):
            return ref.at[pl.ds(mine + n3 * here[a2] + dest, 1)]

        return first, second, third

    stages, directs = {}, {}
    for s in range(len(STREAMS)):
        for k in range(3):
            axis, view, landing = STREAMS[s][k], views(s)[k], landings[k][s]
            if is_ring(s, k):
                stages[s, k] = Ring(s, k, here[axis], place_of[axis], view, landing, send_sem.at[s], sems)
            else:
                directs[s] = sems.take()

    grads_load.wait()
    grads_send.wait_recv()

    def product(pos):
        if pos % 4 == 0:
            wait(lhs.at[pl.ds(pos, 4), pl.ds(0, TOK)], load_sem.at[pos // 4])
        partner_send(pos).wait_recv()
        zl, xj = block(pos)
        total = lax.dot_general(
            lhs[pos], rhs[...], (((0,), (0,)), ((), ())), preferred_element_type=F32
        ).astype(BF16)
        for yi in range(4):
            for zh in range(2):
                at = {"x": xj, "y": yi, "z": zh * 4 + zl}
                rows = total[(yi * 2 + zh) * ROWS : (yi * 2 + zh + 1) * ROWS]
                for s, (a1, a2, a3) in enumerate(STREAMS):
                    for u in range(UNITS[s]):
                        place = (at[a1] * LENGTH[a2] + at[a2]) * LENGTH[a3] + at[a3]
                        partials[s][place, u * 16 : u * 16 + 16] = rows[tile(s, u)]

    sums = jnp.zeros((8, 128), F32)

    def finish(s, total, sums):
        for u in range(UNITS[s]):
            part = total[u * 16 : u * 16 + 16]
            out[tile(s, u)] = part
            sums = sums + part[:8] * part[:8] + part[8:] * part[8:]
        return sums

    order = plan()
    rounds = [t for t in order if t[0] == "l" and t[2] == 0 and STREAMS[t[1]][0] == "z"]
    for t in order:
        if t[0] == "g":
            product(t[1])
        elif t[0] == "d":
            s, axis = t[1], STREAMS[t[1]][2]
            at, odd = here[axis], lax.rem(here[axis], 2)
            away = 2 - 2 * (at // 2)
            for slot, dest in ((0, away + odd), (1, away + 1 - odd)) if t[2] == 0 else ((2, at + 1 - 2 * odd),):
                landing = landings[2][s].at[slot]
                remote(views(s)[2](dest), landing, send_sem.at[s], directs[s], place_of[axis](dest)).start()
        elif t[0] == "s":
            stages[t[1], t[2]].send(*t[3:])
        elif t[2] < 2:
            stages[t[1], t[2]].last(t[3])
        else:
            ring = stages[t[1], 2]
            a, b = ring.arrive(0)
            total = ring.view(ring.me, 0)[0].astype(F32) + a[0].astype(F32)
            sums = finish(t[1], total + b[0].astype(F32), sums)
        if t == rounds[-1]:
            pl.semaphore_signal(heard, inc=1, device_id={"core": other}, device_id_type=MESH_ID)
    for s, sem in directs.items():
        wait(landings[2][s], sem)
        total = views(s)[2](here[STREAMS[s][2]])[0].astype(F32)
        for i in range(LENGTH[STREAMS[s][2]] - 1):
            total = total + landings[2][s][i, 0].astype(F32)
        sums = finish(s, total, sums)
    pl.semaphore_wait(heard, 1)

    def fold(turn, part, offsets, place):
        box = squares.at[turn]
        box[0:1] = part
        for i, off in enumerate(offsets):
            target = box.at[pl.ds(i + 1, 1)]
            remote(box.at[pl.ds(0, 1)], target, fold_sem.at[turn, 0], fold_sem.at[turn, 1], place(off)).start()
        wait(box.at[pl.ds(1, len(offsets))], fold_sem.at[turn, 1])
        return jnp.sum(box[...], axis=0, keepdims=True)

    def along_z(off):
        return {**place_of["z"](lax.rem(here["z"] + off[1], 8)), "core": lax.rem(core + off[0], 2)}

    def across(off):
        return {"x": lax.rem(x + off[0], 4), "y": lax.rem(y + off[1], 4)}

    part = jnp.sum(sums, axis=0, keepdims=True)
    part = fold(0, part, [(c, i) for i in FAR_FIRST[8] for c in (1, 0)][:-1], along_z)
    part = fold(1, part, [(i, k) for i in FAR_FIRST[4] for k in FAR_FIRST[4]][:-1], across)
    total = jnp.sum(part, axis=1, keepdims=True)
    limit = jnp.sqrt(jnp.full((1, 1), float(D * C), F32))
    clip = jnp.minimum(1.0, limit / (jnp.sqrt(total) + 1e-06))
    out[...] = out[...] * clip

    for s, partial in enumerate(partials):
        wait(partial.at[pl.ds(0, 127)], send_sem.at[s])
    for turn in (0, 1):
        wait(squares.at[turn, pl.ds(1, 15)], fold_sem.at[turn, 0])
    wait(lhs.at[:, pl.ds(0, TOK)], in_send.at[0])
    wait(rhs.at[pl.ds(0, TOK)], in_send.at[1])


def scaled_gradient(normed, out_grads):
    landings, sems, many = [], 0, len(STREAMS)
    partials = [pltpu.VMEM((128, units * 16, 128), BF16) for units in UNITS]
    for k in range(3):
        for s in range(many):
            tail = (piece_length(s, k), UNITS[s] * 16, 128)
            if is_ring(s, k):
                slots = len(list(hops(s, k)))
                sems += slots - piece_count(s, k)
            else:
                slots = ring_length(s, k) - 1
                sems += 1
            landings.append(pltpu.VMEM((slots, *tail), BF16))
    return pl.pallas_call(
        kernel,
        out_shape=pltpu.VMEM((ROWS, C), F32),
        in_specs=[pl.BlockSpec(memory_space=pl.ANY)] * 2,
        out_specs=pl.BlockSpec(memory_space=pltpu.VMEM),
        scratch_shapes=[
            pltpu.VMEM((16, 2 * TOK, BLOCK), BF16),
            pltpu.VMEM((2 * TOK, C), BF16),
            *partials,
            *landings,
            pltpu.VMEM((2, 16, 128), F32),
            pltpu.SemaphoreType.DMA((many,)),
            pltpu.SemaphoreType.DMA((sems,)),
            pltpu.SemaphoreType.DMA((5,)),
            pltpu.SemaphoreType.DMA((2,)),
            pltpu.SemaphoreType.DMA((17,)),
            pltpu.SemaphoreType.DMA((2, 2)),
            pltpu.SemaphoreType.REGULAR,
        ],
        compiler_params=pltpu.CompilerParams(collective_id=0, has_side_effects=True),
    )(normed, out_grads)


def shards(normed, out_grads, weight, moment, variance):
    scaled = scaled_gradient(normed, out_grads)
    new_moment = 0.9 * moment + 0.1 * scaled
    new_variance = 0.95 * variance + 0.05 * scaled * scaled
    first = new_moment / (1.0 - 0.9**STEP)
    second = new_variance / (1.0 - 0.95**STEP)
    new_weight = weight - 0.01 * (first / (jnp.sqrt(second) + 1e-08) + 0.1 * weight)
    return (new_weight, new_moment, new_variance)


def solution(mesh):
    split = Mesh(mesh.devices.reshape(SIZES), AXES)
    spec = P(AXES, None)
    return jax.shard_map(
        shards, mesh=split, in_specs=(spec,) * 5, out_specs=(spec,) * 3, check_vma=False
    )
```
